1024 devices in a mesh: ctx: 64 (over x, z), tp: 16 (over y, core).
Axes of the slice: x: 8, y: 8, z: 8, core: 2. Of those that a mesh axis runs over, the one named last changes fastest.
Arguments:
- queries: bfloat16 [16384, 4096], P('ctx', 'tp'), may hold values from -6 to 6
- keys: bfloat16 [16384, 2048], P('ctx', 'tp'), may hold values from -6 to 6
- values: bfloat16 [16384, 2048], P('ctx', 'tp'), may hold values from -6 to 6
- out_weight: bfloat16 [4096, 2688], P('tp'), may hold values from -0.09375 to 0.09375
- out_grad: bfloat16 [16384, 2688], P('ctx'), may hold values from -16 to 16
- block_doc: int32 [64], replicated, may hold values from 0 to 15, never falling along the last dimension, each value on 1 to 10 neighbouring positions
Outputs:
- attn_output: bfloat16 [16384, 2688], P('ctx', 'tp')
- query_grad: bfloat16 [16384, 4096], P('ctx', 'tp')
- key_grad: bfloat16 [16384, 2048], P('ctx', 'tp')
- value_grad: bfloat16 [16384, 2048], P('ctx', 'tp')
- out_weight_grad: float32 [4096, 2688], P('tp', 'ctx')
The draws below stay inside these ranges and needn't reach their ends.
Inputs may be any that keep to these rules, and one draw needn't show every extreme that they name: block_doc never falls; each document covers 1 to 10 whole blocks, one exactly 10.
All inputs are finite; a program needn't handle non-finite values.
Results may differ from the reference program's by a relative error of at most 0.017.
Values may be sent and summed in bfloat16 or wider, within the bound.
A program may use at most 64 MiB of HBM per device.

```python
import math
import jax
import jax.numpy as jnp
import numpy as np
from jax import lax

Q_HEADS = 32
KV_HEADS = 16
HEAD = 128
WINDOW = 1024
D_OUT = 2688
TOK_DEV = 256
TOKENS = 16384
DOCS = 16
DOC_MOST = 10
N_CTX = 64


def base_field(key, width):
    field = jnp.clip(jax.random.normal(jax.random.fold_in(key, 5), (TOKENS, width)), -6.0, 6.0)
    return field.astype(jnp.float32)


def draw_queries(key, part):
    field = base_field(jax.random.fold_in(key, 21), Q_HEADS * HEAD)
    return field.astype(jnp.bfloat16)


def draw_keys(key, part):
    field = base_field(jax.random.fold_in(key, 22), KV_HEADS * HEAD)
    return field.astype(jnp.bfloat16)


def with_spikes(drawn, own_key, source, target, blocks, factor):
    owner, partner = [(jnp.arange(drawn.shape[axis_at]) // (drawn.shape[axis_at] // blocks)).reshape([-1 if axis == axis_at else 1 for axis in range(drawn.ndim)]) for axis_at in (source, target)]
    chosen = jax.random.permutation(own_key, blocks)[partner]
    strong = (owner == chosen) | (owner == (partner + blocks // 2) % blocks)
    return jnp.where(strong, factor * drawn, drawn)


def levels(stream_key, dims, split, low, high):
    factor_of, own = 1.0, jax.random.fold_in(stream_key, 6)
    for dim, shards_of in split:
        draws = jnp.exp(jax.random.uniform(jax.random.fold_in(own, dim), (shards_of,), jnp.float32, low / len(split), high / len(split)))
        factor_of = factor_of * jnp.repeat(draws, dims[dim] // shards_of).reshape([-1 if axis == dim else 1 for axis in range(len(dims))])
    return factor_of


def length_profile(count, total, most, slope):
    weights = [(1 << 20) // math.isqrt(standing ** slope) + 1 for standing in range(2, count + 1)]
    spare, counts = total - most - (count - 1), [1] * (count - 1)
    while spare > 0:
        movable = [i for i in range(count - 1) if counts[i] < most]
        mass, remaining = sum([weights[i] for i in movable]), spare
        for i in movable:
            addition = min(most - counts[i], max(1, remaining * weights[i] // mass), spare)
            counts[i] = counts[i] + addition
            spare = spare - addition
    return np.array([most] + counts)


def ragged(key, number_of, total, most, slope):
    if number_of == 2:
        one = jax.random.randint(key, (), max(1, total - most), min(most, total - 1) + 1)
        return jnp.stack([one, total - one])
    sizes = jnp.asarray(length_profile(number_of, total, most, slope), jnp.int32)
    pairs = (number_of - 1) // 2
    source_of, taker = sizes[1:1 + 2 * pairs:2], sizes[2:2 + 2 * pairs:2]
    slack = jnp.minimum(source_of - 1, most - taker)
    passed = jax.random.randint(jax.random.fold_in(key, 1), (pairs,), 0, 1 << 20) % (slack + 1)
    sizes = sizes.at[1:1 + 2 * pairs:2].set(source_of - passed).at[2:2 + 2 * pairs:2].set(taker + passed)
    return sizes[jax.random.permutation(jax.random.fold_in(key, 2), number_of)]


def normal_values(own_key, extent, scale, bound, split=(), held_as=jnp.bfloat16):
    array = jax.random.normal(own_key, extent, jnp.float32) * scale
    if len(split) > 0:
        array = levels(own_key, extent, split, -0.22, 0.18) * array
    return jnp.clip(array, min=-bound, max=bound).astype(held_as)


def heavy_noise(rng, dims, scale, limit, pieces, heavy, held_as=jnp.bfloat16):
    result = scale * jax.random.normal(rng, dims, jnp.float32)
    if pieces:
        result = result * levels(rng, dims, pieces, -0.22, 0.18)
    return jnp.clip(with_spikes(result, jax.random.fold_in(rng, 3), *heavy), -limit, limit).astype(held_as)


def setup_inputs(seed: int = 0) -> dict:
    arg_keys = jax.random.split(jax.random.key(seed), 7)
    return {
        "queries": draw_queries(jax.random.fold_in(arg_keys[6], 71), 0),
        "keys": draw_keys(jax.random.fold_in(arg_keys[6], 71), 0),
        "values": normal_values(arg_keys[2], (TOKENS, KV_HEADS * HEAD), 1.0, 6.0, ((0, 64), (1, 16))),
        "out_weight": normal_values(arg_keys[3], (Q_HEADS * HEAD, D_OUT), (Q_HEADS * HEAD) ** -0.5, 0.09375, ((0, 16),)),
        "out_grad": heavy_noise(arg_keys[4], (TOKENS, D_OUT), 1.0, 16.0, ((0, 64),), (0, 1, 64, 4.0)),
        "block_doc": jnp.searchsorted(jnp.cumsum(ragged(arg_keys[5], DOCS, N_CTX, DOC_MOST, 2)), jnp.arange(N_CTX), side="right").astype(jnp.int32),
    }


query_scale = 168.0 ** -0.5


def reference(queries, keys, values, out_weight, out_grad, block_doc):
    span_blocks = WINDOW // TOK_DEV
    group_size = Q_HEADS // KV_HEADS
    window_rows = (span_blocks + 1) * TOK_DEV
    lead_rows = span_blocks * TOK_DEV
    key_width = KV_HEADS * HEAD
    key_padded = jnp.concatenate([jnp.zeros((lead_rows, key_width), jnp.bfloat16), keys], axis=0)
    value_padded = jnp.concatenate([jnp.zeros((lead_rows, key_width), jnp.bfloat16), values], axis=0)
    doc_padded = jnp.concatenate([jnp.full((span_blocks,), -1, jnp.int32), block_doc.astype(jnp.int32)])
    rel_key = jnp.arange(window_rows, dtype=jnp.int32)
    rel_query = jnp.arange(TOK_DEV, dtype=jnp.int32) + lead_rows
    near = (rel_key[None, :] <= rel_query[:, None]) & (rel_key[None, :] > rel_query[:, None] - WINDOW)

    def per_block(carry, block):
        key_acc, value_acc = carry
        start = (block * TOK_DEV).astype(jnp.int32)
        zero_index = jnp.zeros((), jnp.int32)
        query_block = lax.dynamic_slice_in_dim(queries, start, TOK_DEV, 0).astype(jnp.float32)
        query_block = query_block.reshape(TOK_DEV, KV_HEADS, group_size, HEAD)
        key_block = lax.dynamic_slice_in_dim(key_padded, start, window_rows, 0).astype(jnp.float32)
        key_block = key_block.reshape(window_rows, KV_HEADS, HEAD)
        value_block = lax.dynamic_slice_in_dim(value_padded, start, window_rows, 0).astype(jnp.float32)
        value_block = value_block.reshape(window_rows, KV_HEADS, HEAD)
        window_docs = lax.dynamic_slice_in_dim(doc_padded, block.astype(jnp.int32), span_blocks + 1, 0)
        key_docs = jnp.repeat(window_docs, TOK_DEV)
        own_doc = lax.dynamic_slice_in_dim(block_doc.astype(jnp.int32), block.astype(jnp.int32), 1, 0)
        visible = near & (key_docs[None, :] == own_doc[0])
        scores = jnp.einsum('tkgd,skd->kgts', query_block, key_block) * query_scale
        scores = jnp.where(visible[None, None], scores, -jnp.inf)
        top = jnp.max(scores, axis=-1, keepdims=True)
        expo = jnp.exp(scores - top)
        probs = expo / jnp.sum(expo, axis=-1, keepdims=True)
        probs_low = probs.astype(jnp.bfloat16).astype(jnp.float32)
        attn = jnp.einsum('kgts,skd->tkgd', probs_low, value_block).astype(jnp.bfloat16)
        grad_rows = lax.dynamic_slice_in_dim(out_grad, start, TOK_DEV, 0)
        d_attn = jnp.dot(grad_rows, out_weight.T, preferred_element_type=jnp.float32).astype(jnp.bfloat16)
        d_attn_h = d_attn.astype(jnp.float32).reshape(TOK_DEV, KV_HEADS, group_size, HEAD)
        d_probs = jnp.einsum('tkgd,skd->kgts', d_attn_h, value_block)
        delta = jnp.einsum('tkgd,tkgd->kgt', attn.astype(jnp.float32), d_attn_h)
        d_scores = (probs * (d_probs - delta[..., None])).astype(jnp.bfloat16).astype(jnp.float32)
        query_grad = (jnp.einsum('kgts,skd->tkgd', d_scores, key_block) * query_scale).astype(jnp.bfloat16)
        key_part = jnp.einsum('kgts,tkgd->skd', d_scores, query_block) * query_scale
        value_part = jnp.einsum('kgts,tkgd->skd', probs_low, d_attn_h)
        key_acc = lax.dynamic_update_slice(key_acc, lax.dynamic_slice_in_dim(key_acc, start, window_rows, 0) + key_part.reshape(window_rows, key_width), (start, zero_index))
        value_acc = lax.dynamic_update_slice(value_acc, lax.dynamic_slice_in_dim(value_acc, start, window_rows, 0) + value_part.reshape(window_rows, key_width), (start, zero_index))
        return (key_acc, value_acc), (attn.reshape(TOK_DEV, Q_HEADS * HEAD), query_grad.reshape(TOK_DEV, Q_HEADS * HEAD))

    initial = (jnp.zeros((TOKENS + lead_rows, key_width), jnp.float32), jnp.zeros((TOKENS + lead_rows, key_width), jnp.float32))
    (key_acc, value_acc), (attn_blocks, qgrad_blocks) = lax.scan(per_block, initial, jnp.arange(TOKENS // TOK_DEV, dtype=jnp.int32))
    attn_all = attn_blocks.reshape(TOKENS, Q_HEADS * HEAD)
    attn_output = jnp.dot(attn_all, out_weight, preferred_element_type=jnp.float32).astype(jnp.bfloat16)
    out_weight_grad = jnp.dot(attn_all.T, out_grad, preferred_element_type=jnp.float32)
    query_grad = qgrad_blocks.reshape(TOKENS, Q_HEADS * HEAD)
    key_grad = key_acc[lead_rows:].astype(jnp.bfloat16)
    value_grad = value_acc[lead_rows:].astype(jnp.bfloat16)
    return (attn_output, query_grad, key_grad, value_grad, out_weight_grad)
```

```python
import functools
import math

import jax
import jax.numpy as jnp
from jax import lax
from jax.experimental import pallas as pl
from jax.experimental.pallas import tpu as pltpu
from jax.sharding import PartitionSpec as P

MESH = pl.DeviceIdType.MESH
HEAD = 128
HEADS = 2
REACH = 4
query_scale = 168.0 ** -0.5
EXPONENT = query_scale * math.log2(math.e)
HIDDEN = -1e30
F32, BF16 = jnp.float32, jnp.bfloat16


def dot(a, b, a_dim, b_dim):
    return lax.dot_general(a, b, (((a_dim,), (b_dim,)), ((), ())), preferred_element_type=F32)


def ring_slots(n):
    length = {}
    for half in (0, 1):
        far, near = n // 2, n - 1 - n // 2
        length[half, 1] = far if half == 0 else near
        length[half, -1] = near if half == 0 else far
    slot = {}
    for key, steps in length.items():
        for step in range(1, steps + 1):
            slot[key + (step,)] = len(slot)
    return slot, length


def kernel(nx, ny, nz, doc, q_in, k_in, v_in, w_in, g_in, out_o, dq_o, dk_o, dv_o, dw_o, *scratch):
    (q_s, k_s, v_s, w_s, g_s, wt_s, gt_s, p_s, dp_s, at_s, do_s, dot_s, xs, xr, ys, yr, gs, gr,
     za, zf, zs, zr, ya, cs, cr,
     load_sem, k_snd, k_rcv, v_snd, v_rcv, x_snd, x_rcv, y_snd, y_rcv, g_snd, g_rcv, z_snd, z_rcv, c_snd, c_rcv) = scratch
    n_ctx = nx * nz
    ctx, tp = lax.axis_index("ctx"), lax.axis_index("tp")
    x, z = ctx // nz, ctx % nz
    y, core = tp // 2, tp % 2
    following, preceding = ((ctx + 1) % n_ctx, tp), ((ctx + n_ctx - 1) % n_ctx, tp)
    x_next = {1: ((x + 1) % nx * nz + z, tp), -1: ((x + nx - 1) % nx * nz + z, tp)}
    y_next = {1: (ctx, (y + 1) % ny * 2 + core), -1: (ctx, (y + ny - 1) % ny * 2 + core)}
    partner = (ctx, y * 2 + 1 - core)
    z_peer = {o: (x * nz + (z + o) % nz, tp) for o in range(1, nz)}
    chunk_x, chunk_y = gt_s.shape[0] // nx, wt_s.shape[0] // ny
    piece = chunk_x // nz

    loads = [pltpu.make_async_copy(src, dst, load_sem.at[i]) for i, (src, dst) in enumerate(
        [(k_in, k_s.at[0]), (q_in, q_s), (v_in, v_s.at[0]), (g_in, g_s), (w_in, w_s)])]
    for load in loads:
        load.start()
    barrier = pltpu.get_barrier_semaphore()
    greeted = [following, preceding, *x_next.values(), *y_next.values(), partner, *z_peer.values()]
    for device in greeted:
        pl.semaphore_signal(barrier, inc=1, device_id=device, device_id_type=MESH)
    pl.semaphore_wait(barrier, len(greeted))

    def send(src, dst, snd, rcv, device):
        copy = pltpu.make_async_remote_copy(src_ref=src, dst_ref=dst, send_sem=snd, recv_sem=rcv, device_id=device,
                                            device_id_type=MESH)
        copy.start()
        return copy

    k_copy, v_copy = {}, {}

    def pass_k(d):
        k_copy[d] = send(k_in if d == 0 else k_s.at[d], k_s.at[d + 1], k_snd.at[d], k_rcv.at[d], following)

    def pass_v(d):
        v_copy[d] = send(v_in if d == 0 else v_s.at[d], v_s.at[d + 1], v_snd.at[d], v_rcv.at[d], following)

    pass_k(0)
    pass_v(0)

    own_doc = doc[ctx]
    bias = [None] + [
        jnp.where((ctx >= d) & (doc[(ctx + n_ctx - d) % n_ctx] == own_doc), 0.0, HIDDEN).astype(F32)
        for d in range(1, REACH + 1)
    ]
    size = q_s.shape[0]
    key_at = lax.broadcasted_iota(jnp.int32, (size, size), 0)
    query_at = lax.broadcasted_iota(jnp.int32, (size, size), 1)

    def head(ref, h):
        return ref[:, h * HEAD:(h + 1) * HEAD]

    top, top_at, total, acc = {}, {}, {}, {}

    def attend(d):
        for h in range(HEADS):
            s = dot(k_s[d], head(q_s, h), 1, 1)
            if d == 0:
                s = jnp.where(key_at <= query_at, s, HIDDEN)
            if d == REACH:
                s = jnp.where(key_at > query_at, s, HIDDEN)
            most = jnp.max(s, axis=0, keepdims=True) * EXPONENT
            if d > 0:
                most = jnp.maximum(top[h], most + bias[d])
            p = jnp.exp2(s * EXPONENT - (most if d == 0 else most - bias[d]))
            p_s[d, h] = p
            rows = jnp.sum(p, axis=0, keepdims=True)
            if d == 0:
                total[h] = rows
            else:
                fade = jnp.exp2(top[h] - most)
                total[h] = total[h] * fade + rows
                acc[h] = acc[h] * fade
            top[h] = top_at[d, h] = most

    def weigh(d):
        for h in range(HEADS):
            part = dot(v_s[d], p_s[d, h].astype(BF16), 0, 0)
            acc[h] = part if d == 0 else acc[h] + part

    def value_side(d):
        for h in range(HEADS):
            dp_s[d, h] = dot(v_s[d], head(do_s, h), 1, 1)

    def turn(src, dst):
        for j in range(src.shape[1] // 128):
            dst[j * 128:(j + 1) * 128, :] = src[:, j * 128:(j + 1) * 128].T

    for load in loads[:3]:
        load.wait()
    attend(0)
    weigh(0)
    for load in loads[3:]:
        load.wait()
    do_s[...] = dot(g_s[...], w_s[...], 1, 1).astype(BF16)
    for d in range(1, REACH + 1):
        k_copy[d - 1].wait_recv()
        if d < REACH:
            pass_k(d)
        if d > 1:
            attend(d)
        v_copy[d - 1].wait_recv()
        if d < REACH:
            pass_v(d)
        if d == 1:
            attend(d)
            dot_s[...] = dot(w_s[...], g_s[...], 1, 1).astype(BF16)
        weigh(d)
        if d == 1:
            value_side(0)
            value_side(1)
        elif d < REACH:
            value_side(d)
        if d == 2:
            turn(g_s, gt_s)
        if d == 3:
            turn(w_s, wt_s)

    share, delta = {}, {}
    for h in range(HEADS):
        share[h] = 1.0 / total[h]
        attn = (acc[h] * share[h]).astype(BF16)
        at_s[h * HEAD:(h + 1) * HEAD, :] = attn
        delta[h] = jnp.sum(attn.astype(F32) * dot_s[h * HEAD:(h + 1) * HEAD, :].astype(F32), axis=0, keepdims=True)

    def weight_term(at, half):
        rows = gt_s[pl.ds(pl.multiple_of(at * chunk_x, 16), chunk_x), :]
        return dot(rows, at_s[half * 128:(half + 1) * 128, :], 1, 1)

    def output_term(at, half):
        rows = wt_s[pl.ds(pl.multiple_of(at * chunk_y, 16), chunk_y), :]
        return dot(rows, at_s[:, half * 128:(half + 1) * 128], 1, 0)

    x_slot, x_len = ring_slots(nx)
    y_slot, y_len = ring_slots(ny)
    chains = {"x": (weight_term, x, nx, x_next, xs, xr, x_snd, x_rcv, x_slot, x_len, {}),
              "y": (output_term, y, ny, y_next, ys, yr, y_snd, y_rcv, y_slot, y_len, {})}

    def chain_step(name, step):
        term, me, n, neighbour, out, arrived, snd, rcv, slot, length, copies = chains[name]
        for half in (0, 1):
            for way in (1, -1):
                if step > length[half, way]:
                    continue
                at = (me + n + way * (length[half, way] - step + 1)) % n
                part = term(at, half)
                if step > 1:
                    before = half, way, step - 1
                    copies[before].wait_recv()
                    part = part + arrived[slot[before]].astype(F32)
                now = slot[half, way, step]
                out[now] = part.astype(BF16)
                copies[half, way, step] = send(out.at[now], arrived.at[now], snd.at[now], rcv.at[now], neighbour[way])

    def chain_end(name, half):
        term, me, n, neighbour, out, arrived, snd, rcv, slot, length, copies = chains[name]
        part = term(me, half)
        for way in (1, -1):
            steps = length[half, way]
            if steps:
                copies[half, way, steps].wait_recv()
                part = part + arrived[slot[half, way, steps]].astype(F32)
        return part

    query_part, grad_copies = {}, {}

    def backward(d):
        key_part = value_part = None
        for h in range(HEADS):
            probs = p_s[d, h] * (jnp.exp2(top_at[d, h] - top[h]) * share[h])
            d_scores = (probs * (dp_s[d, h] - delta[h])).astype(BF16)
            to_value = dot(probs.astype(BF16), head(do_s, h), 1, 0)
            to_key = dot(d_scores, head(q_s, h), 1, 0)
            to_query = dot(k_s[d], d_scores, 0, 0)
            query_part[h] = query_part[h] + to_query if h in query_part else to_query
            key_part = to_key if key_part is None else key_part + to_key
            value_part = to_value if value_part is None else value_part + to_value
        return key_part, value_part

    def grad_step(step):
        parts = backward(REACH + 1 - step)
        for kind in (0, 1):
            part = parts[kind]
            if step > 1:
                grad_copies[step - 1, kind].wait_recv()
                part = part + gr[step - 2, kind].astype(F32)
            gs[step - 1, kind] = part.astype(BF16)
            grad_copies[step, kind] = send(gs.at[step - 1, kind], gr.at[step - 1, kind], g_snd.at[step - 1, kind],
                                           g_rcv.at[step - 1, kind], preceding)

    steps_x, steps_y = max(x_len.values()), max(y_len.values())
    for step in range(1, max(steps_x, steps_y, REACH) + 1):
        if step <= steps_x:
            chain_step("x", step)
        if step <= steps_y:
            chain_step("y", step)
        if step == 1:
            value_side(REACH)
        if step <= REACH:
            grad_step(step)

    z_copies = {}
    for half in (0, 1):
        za[0:chunk_x, :] = chain_end("x", half)
        za[chunk_x:, :] = jnp.zeros((za.shape[0] - chunk_x, 128), F32)
        for i in range(nz):
            rows = za[i * piece:i * piece + zf.shape[2], :]
            zf[half, i] = rows
            zs[half, i] = rows.astype(BF16)
        for o in sorted(range(1, nz), key=lambda o: -min(o, nz - o)):
            z_copies[half, o] = send(zs.at[half, (z + o) % nz], zr.at[half, o - 1], z_snd.at[half, o - 1],
                                     z_rcv.at[half, o - 1], z_peer[o])
    for half in (0, 1):
        ya[:, half * 128:(half + 1) * 128] = chain_end("y", half)
    mine = chunk_y // 2
    cs[...] = ya[pl.ds(pl.multiple_of((1 - core) * mine, 8), mine), :].astype(BF16)
    core_copy = send(cs, cr, c_snd, c_rcv, partner)

    key_part, value_part = backward(0)
    for h in range(HEADS):
        dq_o[h * HEAD:(h + 1) * HEAD, :] = (query_part[h] * query_scale).astype(BF16)
    grad_copies[REACH, 0].wait_recv()
    dk_o[...] = ((key_part + gr[REACH - 1, 0].astype(F32)) * query_scale).astype(BF16)
    grad_copies[REACH, 1].wait_recv()
    dv_o[...] = (value_part + gr[REACH - 1, 1].astype(F32)).astype(BF16)
    core_copy.wait_recv()
    out_o[...] = (ya[pl.ds(pl.multiple_of(core * mine, 8), mine), :] + cr[...].astype(F32)).astype(BF16)
    for half in (0, 1):
        part = zf[half, z]
        for o in range(1, nz):
            z_copies[half, o].wait_recv()
            part = part + zr[half, o - 1].astype(F32)
        dw_o[:, half * 128:(half + 1) * 128] = part
    for copies in (k_copy, v_copy, chains["x"][-1], chains["y"][-1], grad_copies, z_copies, {0: core_copy}):
        for copy in copies.values():
            copy.wait_send()


def local(nx, ny, nz, queries, keys, values, out_weight, out_grad, block_doc):
    size, width = queries.shape
    features = out_weight.shape[1]
    chunk_x, chunk_y = features // nx, features // ny
    piece = chunk_x // nz
    piece_rows = -(-piece // 16) * 16
    x_slots, y_slots = len(ring_slots(nx)[0]), len(ring_slots(ny)[0])
    DMA = pltpu.SemaphoreType.DMA
    V = pltpu.VMEM
    scratch = [
        V((size, width), BF16), V((REACH + 1, size, HEAD), BF16), V((REACH + 1, size, HEAD), BF16),
        V((width, features), BF16), V((size, features), BF16), V((features, width), BF16), V((features, size), BF16),
        V((REACH + 1, HEADS, size, size), F32), V((REACH + 1, HEADS, size, size), F32),
        V((width, size), BF16), V((size, width), BF16), V((width, size), BF16),
        V((x_slots, chunk_x, 128), BF16), V((x_slots, chunk_x, 128), BF16),
        V((y_slots, chunk_y, 128), BF16), V((y_slots, chunk_y, 128), BF16),
        V((REACH, 2, size, HEAD), BF16), V((REACH, 2, size, HEAD), BF16),
        V((chunk_x + piece_rows, 128), F32), V((2, nz, piece_rows, 128), F32), V((2, nz, piece_rows, 128), BF16),
        V((2, max(nz - 1, 1), piece_rows, 128), BF16),
        V((chunk_y, size), F32), V((chunk_y // 2, size), BF16), V((chunk_y // 2, size), BF16),
        DMA((5,)), DMA((REACH,)), DMA((REACH,)), DMA((REACH,)), DMA((REACH,)),
        DMA((x_slots,)), DMA((x_slots,)), DMA((y_slots,)), DMA((y_slots,)),
        DMA((REACH, 2)), DMA((REACH, 2)), DMA((2, nz - 1)), DMA((2, nz - 1)), DMA, DMA,
    ]
    anywhere, vmem = pl.BlockSpec(memory_space=pl.ANY), pl.BlockSpec(memory_space=pltpu.VMEM)
    out, dq, dk, dv, dw = pl.pallas_call(
        functools.partial(kernel, nx, ny, nz),
        out_shape=[
            jax.ShapeDtypeStruct((chunk_y // 2, size), BF16),
            jax.ShapeDtypeStruct((width, size), BF16),
            jax.ShapeDtypeStruct((size, HEAD), BF16),
            jax.ShapeDtypeStruct((size, HEAD), BF16),
            jax.ShapeDtypeStruct((piece_rows, width), F32),
        ],
        in_specs=[pl.BlockSpec(memory_space=pltpu.SMEM)] + [anywhere] * 5,
        out_specs=[vmem] * 5,
        scratch_shapes=scratch,
        compiler_params=pltpu.CompilerParams(collective_id=0, has_side_effects=True),
        name="layer",
    )(block_doc, queries, keys, values, out_weight, out_grad)
    return out.T, dq.T, dk, dv, dw[:piece].T


def solution(mesh, nx=8, ny=8, nz=8):
    placed = (P("ctx", "tp"), P("ctx", "tp"), P("ctx", "tp"), P("tp", None), P("ctx", None), P())
    return jax.shard_map(
        functools.partial(local, nx, ny, nz),
        mesh=mesh,
        in_specs=placed,
        out_specs=(P("ctx", "tp"), P("ctx", "tp"), P("ctx", "tp"), P("ctx", "tp"), P("tp", "ctx")),
        check_vma=False,
    )
```

```python
import functools
import math

import jax
import jax.numpy as jnp
from jax import lax
from jax.experimental import pallas as pl
from jax.experimental.pallas import tpu as pltpu
from jax.sharding import PartitionSpec as P

MESH = pl.DeviceIdType.MESH
HEAD = 128
HEADS = 2
REACH = 4
query_scale = 168.0 ** -0.5
EXPONENT = query_scale * math.log2(math.e)
HIDDEN = -1e30
F32, BF16 = jnp.float32, jnp.bfloat16


def dot(a, b, a_dim, b_dim):
    return lax.dot_general(a, b, (((a_dim,), (b_dim,)), ((), ())), preferred_element_type=F32)


def ring_slots(n):
    length = {}
    for half in (0, 1):
        far, near = n // 2, n - 1 - n // 2
        length[half, 1] = far if half == 0 else near
        length[half, -1] = near if half == 0 else far
    slot = {}
    for key, steps in length.items():
        for step in range(1, steps + 1):
            slot[key + (step,)] = len(slot)
    return slot, length


def kernel(nx, ny, nz, doc, q_in, k_in, v_in, w_in, g_in, out_o, dq_o, dk_o, dv_o, dw_o, *scratch):
    (q_s, k_s, v_s, w_s, g_s, wt_s, gt_s, p_s, dp_s, at_s, do_s, dot_s, xs, xr, ys, yr, gs, gr,
     za, zf, zs, zr, ya, ls, lr, cs, cr,
     load_sem, k_snd, k_rcv, v_snd, v_rcv, x_snd, x_rcv, y_snd, y_rcv, g_snd, g_rcv, z_snd, z_rcv, l_snd, l_rcv, c_snd, c_rcv) = scratch
    n_ctx = nx * nz
    ctx, tp = lax.axis_index("ctx"), lax.axis_index("tp")
    x, z = ctx // nz, ctx % nz
    y, core = tp // 2, tp % 2
    following, preceding = ((ctx + 1) % n_ctx, tp), ((ctx + n_ctx - 1) % n_ctx, tp)
    x_next = {1: ((x + 1) % nx * nz + z, tp), -1: ((x + nx - 1) % nx * nz + z, tp)}
    y_next = {1: (ctx, (y + 1) % ny * 2 + core), -1: (ctx, (y + ny - 1) % ny * 2 + core)}
    partner = (ctx, y * 2 + 1 - core)
    y_across = [(ctx, (y + way) % ny * 2 + 1 - core) for way in (1, ny - 1)]
    z_peer = {o: (x * nz + (z + o) % nz, tp) for o in range(1, nz)}
    chunk_x, chunk_y = gt_s.shape[0] // nx, wt_s.shape[0] // ny
    piece = chunk_x // nz

    loads = [pltpu.make_async_copy(src, dst, load_sem.at[i]) for i, (src, dst) in enumerate(
        [(k_in, k_s.at[0]), (q_in, q_s), (v_in, v_s.at[0]), (g_in, g_s), (w_in, w_s)])]
    for load in loads:
        load.start()
    barrier = pltpu.get_barrier_semaphore()
    greeted = [following, preceding, *x_next.values(), *y_next.values(), *y_across, partner, *z_peer.values()]
    for device in greeted:
        pl.semaphore_signal(barrier, inc=1, device_id=device, device_id_type=MESH)
    pl.semaphore_wait(barrier, len(greeted))

    def send(src, dst, snd, rcv, device):
        copy = pltpu.make_async_remote_copy(src_ref=src, dst_ref=dst, send_sem=snd, recv_sem=rcv, device_id=device,
                                            device_id_type=MESH)
        copy.start()
        return copy

    k_copy, v_copy = {}, {}

    def pass_k(d):
        k_copy[d] = send(k_in if d == 0 else k_s.at[d], k_s.at[d + 1], k_snd.at[d], k_rcv.at[d], following)

    def pass_v(d):
        v_copy[d] = send(v_in if d == 0 else v_s.at[d], v_s.at[d + 1], v_snd.at[d], v_rcv.at[d], following)

    pass_k(0)

    own_doc = doc[ctx]
    bias = [None] + [
        jnp.where((ctx >= d) & (doc[(ctx + n_ctx - d) % n_ctx] == own_doc), 0.0, HIDDEN).astype(F32)
        for d in range(1, REACH + 1)
    ]
    size = q_s.shape[0]
    key_at = lax.broadcasted_iota(jnp.int32, (size, size), 0)
    query_at = lax.broadcasted_iota(jnp.int32, (size, size), 1)

    def head(ref, h):
        return ref[:, h * HEAD:(h + 1) * HEAD]

    top, top_at, total, acc = {}, {}, {}, {}

    def attend(d):
        for h in range(HEADS):
            s = dot(k_s[d], head(q_s, h), 1, 1)
            if d == 0:
                s = jnp.where(key_at <= query_at, s, HIDDEN)
            if d == REACH:
                s = jnp.where(key_at > query_at, s, HIDDEN)
            most = jnp.max(s, axis=0, keepdims=True) * EXPONENT
            if d > 0:
                most = jnp.maximum(top[h], most + bias[d])
            p = jnp.exp2(s * EXPONENT - (most if d == 0 else most - bias[d]))
            p_s[d, h] = p
            rows = jnp.sum(p, axis=0, keepdims=True)
            if d == 0:
                total[h] = rows
            else:
                fade = jnp.exp2(top[h] - most)
                total[h] = total[h] * fade + rows
                acc[h] = acc[h] * fade
            top[h] = top_at[d, h] = most

    def weigh(d, heads=range(HEADS)):
        for h in heads:
            part = dot(v_s[d], p_s[d, h].astype(BF16), 0, 0)
            acc[h] = part if d == 0 else acc[h] + part

    def value_side(d):
        for h in range(HEADS):
            dp_s[d, h] = dot(v_s[d], head(do_s, h), 1, 1)

    def turn(src, dst):
        for j in range(src.shape[1] // 128):
            dst[j * 128:(j + 1) * 128, :] = src[:, j * 128:(j + 1) * 128].T

    for load in loads[:2]:
        load.wait()
    attend(0)
    k_copy[0].wait_send()
    pass_v(0)
    for load in loads[2:]:
        load.wait()
    weigh(0)
    do_s[...] = dot(g_s[...], w_s[...], 1, 1).astype(BF16)
    for d in range(1, REACH + 1):
        k_copy[d - 1].wait_recv()
        if d < REACH:
            pass_k(d)
        attend(d)
        v_copy[d - 1].wait_recv()
        if d < REACH:
            pass_v(d)
            weigh(d)
            if d == 1:
                dot_s[...] = dot(w_s[...], g_s[...], 1, 1).astype(BF16)
                value_side(0)
            value_side(d)
            if d == 2:
                turn(g_s, gt_s)
            if d == 3:
                turn(w_s, wt_s)

    share, delta = {}, {}

    def conclude(h):
        weigh(REACH, [h])
        share[h] = 1.0 / total[h]
        attn = (acc[h] * share[h]).astype(BF16)
        at_s[h * HEAD:(h + 1) * HEAD, :] = attn
        delta[h] = jnp.sum(attn.astype(F32) * dot_s[h * HEAD:(h + 1) * HEAD, :].astype(F32), axis=0, keepdims=True)

    def weight_term(at, half):
        rows = gt_s[pl.ds(pl.multiple_of(at * chunk_x, 16), chunk_x), :]
        return dot(rows, at_s[half * 128:(half + 1) * 128, :], 1, 1)

    def output_term(at, half):
        rows = wt_s[pl.ds(pl.multiple_of(at * chunk_y, 16), chunk_y), :]
        return dot(rows, at_s[:, half * 128:(half + 1) * 128], 1, 0)

    x_slot, x_len = ring_slots(nx)
    y_slot, y_len = ring_slots(ny)
    chains = {"x": (weight_term, x, nx, x_next, xs, xr, x_snd, x_rcv, x_slot, x_len, {}),
              "y": (output_term, y, ny, y_next, ys, yr, y_snd, y_rcv, y_slot, y_len, {})}

    last_copies = {}

    def chain_step(name, half, step):
        term, me, n, neighbour, out, arrived, snd, rcv, slot, length, copies = chains[name]
        for way in (1, -1):
            if step > length[half, way]:
                continue
            at = (me + n + way * (length[half, way] - step + 1)) % n
            part = term(at, half)
            if step > 1:
                before = half, way, step - 1
                copies[before].wait_recv()
                part = part + arrived[slot[before]].astype(F32)
            if name == "y" and step == length[half, way]:
                side = (1 - way) // 2
                for to in (0, 1):
                    ls[half, side, to] = part[to * mine:(to + 1) * mine].astype(BF16)
                    last_copies[half, side, to] = send(
                        ls.at[half, side, to], lr.at[half, side, core], l_snd.at[half, side, to],
                        l_rcv.at[half, side, core], (ctx, (y + ny + way) % ny * 2 + to))
                continue
            now = slot[half, way, step]
            out[now] = part.astype(BF16)
            copies[half, way, step] = send(out.at[now], arrived.at[now], snd.at[now], rcv.at[now], neighbour[way])

    def weight_end(half):
        term, me, n, neighbour, out, arrived, snd, rcv, slot, length, copies = chains["x"]
        part = term(me, half)
        for way in (1, -1):
            steps = length[half, way]
            if steps:
                copies[half, way, steps].wait_recv()
                part = part + arrived[slot[half, way, steps]].astype(F32)
        return part

    def output_end(half):
        columns = slice(half * 128, (half + 1) * 128)
        part = ya[pl.ds(pl.multiple_of(core * mine, 8), mine), columns] + cr[:, columns].astype(F32)
        for way in (1, -1):
            if y_len[half, way]:
                for source in (0, 1):
                    side = (1 - way) // 2
                    pltpu.make_async_remote_copy(
                        src_ref=ls.at[half, side, 0], dst_ref=lr.at[half, side, source], send_sem=l_snd.at[half, side, 0],
                        recv_sem=l_rcv.at[half, side, source], device_id=partner, device_id_type=MESH).wait_recv()
                    part = part + lr[half, side, source].astype(F32)
        out_o[:, columns] = part.astype(BF16)

    query_part, grad_copies = {}, {}

    def backward(d):
        key_part = value_part = None
        for h in range(HEADS):
            probs = p_s[d, h] * (jnp.exp2(top_at[d, h] - top[h]) * share[h])
            d_scores = (probs * (dp_s[d, h] - delta[h])).astype(BF16)
            to_value = dot(probs.astype(BF16), head(do_s, h), 1, 0)
            to_key = dot(d_scores, head(q_s, h), 1, 0)
            to_query = dot(k_s[d], d_scores, 0, 0)
            query_part[h] = query_part[h] + to_query if h in query_part else to_query
            key_part = to_key if key_part is None else key_part + to_key
            value_part = to_value if value_part is None else value_part + to_value
        return key_part, value_part

    def grad_step(step, kind, part):
        if step > 1:
            grad_copies[step - 1, kind].wait_recv()
            part = part + gr[step - 2, kind].astype(F32)
        gs[step - 1, kind] = part.astype(BF16)
        grad_copies[step, kind] = send(gs.at[step - 1, kind], gr.at[step - 1, kind], g_snd.at[step - 1, kind],
                                       g_rcv.at[step - 1, kind], preceding)

    mine = chunk_y // 2
    steps_x, steps_y = max(x_len.values()), max(y_len.values())
    for step in range(1, max(steps_x, steps_y, REACH) + 1):
        if step == 1:
            conclude(0)
        if step <= steps_x:
            chain_step("x", 0, step)
        if step == 1:
            conclude(1)
        if step <= steps_y:
            chain_step("y", 0, step)
        if step == 1:
            value_side(REACH)
        if step <= REACH:
            key_part, value_part = backward(REACH + 1 - step)
            grad_step(step, 0, key_part)
        if step <= steps_x:
            chain_step("x", 1, step)
        if step <= steps_y:
            chain_step("y", 1, step)
        if step <= REACH:
            grad_step(step, 1, value_part)
        if step == 1:
            for half in (0, 1):
                ya[:, half * 128:(half + 1) * 128] = output_term(y, half)
            cs[...] = ya[pl.ds(pl.multiple_of((1 - core) * mine, 8), mine), :].astype(BF16)
            core_copy = send(cs, cr, c_snd, c_rcv, partner)

    key_part, value_part = backward(0)
    for h in range(HEADS):
        dq_o[:, h * HEAD:(h + 1) * HEAD] = (query_part[h] * query_scale).T.astype(BF16)
    z_copies = {}
    za[chunk_x:, :] = jnp.zeros((za.shape[0] - chunk_x, 128), F32)
    for half in (0, 1):
        za[0:chunk_x, :] = weight_end(half)
        for i in range(nz):
            rows = za[i * piece:i * piece + zf.shape[2], :]
            zf[half, i] = rows
            zs[half, i] = rows.astype(BF16)
        for o in sorted(range(1, nz), key=lambda o: -min(o, nz - o)):
            z_copies[half, o] = send(zs.at[half, (z + o) % nz], zr.at[half, o - 1], z_snd.at[half, o - 1],
                                     z_rcv.at[half, o - 1], z_peer[o])
    core_copy.wait_recv()
    output_end(0)
    output_end(1)
    grad_copies[REACH, 0].wait_recv()
    dk_o[...] = ((key_part + gr[REACH - 1, 0].astype(F32)) * query_scale).astype(BF16)
    grad_copies[REACH, 1].wait_recv()
    dv_o[...] = (value_part + gr[REACH - 1, 1].astype(F32)).astype(BF16)
    for half in (0, 1):
        part = zf[half, z]
        for o in range(1, nz):
            z_copies[half, o].wait_recv()
            part = part + zr[half, o - 1].astype(F32)
        dw_o[:, half * 128:(half + 1) * 128] = part[:piece]
    del k_copy[0]
    for copies in (k_copy, v_copy, chains["x"][-1], chains["y"][-1], grad_copies, last_copies, z_copies, {0: core_copy}):
        for copy in copies.values():
            copy.wait_send()


def hand_over(*refs):
    for src, dst in zip(refs[:5], refs[5:]):
        dst[...] = src[...]


def local(nx, ny, nz, queries, keys, values, out_weight, out_grad, block_doc):
    size, width = queries.shape
    features = out_weight.shape[1]
    chunk_x, chunk_y = features // nx, features // ny
    piece = chunk_x // nz
    piece_rows = -(-piece // 16) * 16
    x_slots, y_slots = len(ring_slots(nx)[0]), len(ring_slots(ny)[0])
    DMA = pltpu.SemaphoreType.DMA
    V = pltpu.VMEM
    scratch = [
        V((size, width), BF16), V((REACH + 1, size, HEAD), BF16), V((REACH + 1, size, HEAD), BF16),
        V((width, features), BF16), V((size, features), BF16), V((features, width), BF16), V((features, size), BF16),
        V((REACH + 1, HEADS, size, size), F32), V((REACH + 1, HEADS, size, size), F32),
        V((width, size), BF16), V((size, width), BF16), V((width, size), BF16),
        V((x_slots, chunk_x, 128), BF16), V((x_slots, chunk_x, 128), BF16),
        V((y_slots, chunk_y, 128), BF16), V((y_slots, chunk_y, 128), BF16),
        V((REACH, 2, size, HEAD), BF16), V((REACH, 2, size, HEAD), BF16),
        V((chunk_x + piece_rows, 128), F32), V((2, nz, piece_rows, 128), F32), V((2, nz, piece_rows, 128), BF16),
        V((2, max(nz - 1, 1), piece_rows, 128), BF16),
        V((chunk_y, size), F32), V((2, 2, 2, chunk_y // 2, 128), BF16), V((2, 2, 2, chunk_y // 2, 128), BF16),
        V((chunk_y // 2, size), BF16), V((chunk_y // 2, size), BF16),
        DMA((5,)), DMA((REACH,)), DMA((REACH,)), DMA((REACH,)), DMA((REACH,)),
        DMA((x_slots,)), DMA((x_slots,)), DMA((y_slots,)), DMA((y_slots,)),
        DMA((REACH, 2)), DMA((REACH, 2)), DMA((2, nz - 1)), DMA((2, nz - 1)),
        DMA((2, 2, 2)), DMA((2, 2, 2)), DMA, DMA,
    ]
    in_hbm, vmem = pl.BlockSpec(memory_space=pltpu.HBM), pl.BlockSpec(memory_space=pltpu.VMEM)
    results = pl.pallas_call(
        functools.partial(kernel, nx, ny, nz),
        out_shape=[
            jax.ShapeDtypeStruct((chunk_y // 2, size), BF16),
            jax.ShapeDtypeStruct((size, width), BF16),
            jax.ShapeDtypeStruct((size, HEAD), BF16),
            jax.ShapeDtypeStruct((size, HEAD), BF16),
            jax.ShapeDtypeStruct((piece, width), F32),
        ],
        in_specs=[pl.BlockSpec(memory_space=pltpu.SMEM)] + [in_hbm] * 5,
        out_specs=[vmem] * 5,
        scratch_shapes=scratch,
        compiler_params=pltpu.CompilerParams(collective_id=0, has_side_effects=True, vmem_limit_bytes=40 << 20),
        name="layer",
    )(*[pltpu.with_memory_space_constraint(a, pltpu.HBM) for a in (block_doc, queries, keys, values, out_weight, out_grad)])
    out, dq, dk, dv, dw = pl.pallas_call(
        hand_over,
        out_shape=[jax.ShapeDtypeStruct(r.shape, r.dtype) for r in results],
        in_specs=[vmem] * 5,
        out_specs=[vmem] * 5,
        compiler_params=pltpu.CompilerParams(vmem_limit_bytes=8 << 20),
        name="hand_over",
    )(*results)
    return out.T, dq, dk, dv, dw.T


def solution(mesh, nx=8, ny=8, nz=8):
    placed = (P("ctx", "tp"), P("ctx", "tp"), P("ctx", "tp"), P("tp", None), P("ctx", None), P())
    return jax.shard_map(
        functools.partial(local, nx, ny, nz),
        mesh=mesh,
        in_specs=placed,
        out_specs=(P("ctx", "tp"), P("ctx", "tp"), P("ctx", "tp"), P("ctx", "tp"), P("tp", "ctx")),
        check_vma=False,
    )
```

```python
import functools
import math

import jax
import jax.numpy as jnp
from jax import lax
from jax.experimental import pallas as pl
from jax.experimental.pallas import tpu as pltpu
from jax.sharding import PartitionSpec as P

MESH = pl.DeviceIdType.MESH
HEAD = 128
HEADS = 2
REACH = 4
query_scale = 168.0 ** -0.5
EXPONENT = query_scale * math.log2(math.e)
HIDDEN = -1e30
F32, BF16 = jnp.float32, jnp.bfloat16


def dot(a, b, a_dim, b_dim):
    return lax.dot_general(a, b, (((a_dim,), (b_dim,)), ((), ())), preferred_element_type=F32)


def ring_slots(n):
    length = {}
    for half in (0, 1):
        far, near = n // 2, n - 1 - n // 2
        length[half, 1] = far if half == 0 else near
        length[half, -1] = near if half == 0 else far
    slot = {}
    for key, steps in length.items():
        for step in range(1, steps + 1):
            slot[key + (step,)] = len(slot)
    return slot, length


def kernel(nx, ny, nz, doc_in, q_in, k_in, v_in, w_in, g_in, out_o, dq_o, dk_o, dv_o, dw_o, *scratch):
    (doc, q_s, k_s, v_s, w_s, g_s, wf_s, wt_s, gt_s, p_s, dp_s, at_s, do_s, dot_s, xs, xr, ys, yr, gs, gr,
     za, zf, zs, zr, cs, cr,
     load_sem, k_snd, k_rcv, v_snd, v_rcv, x_snd, x_rcv, y_snd, y_rcv, g_snd, g_rcv, z_snd, z_rcv, c_snd, c_rcv, z_ready) = scratch
    n_ctx = nx * nz
    ctx, tp = lax.axis_index("ctx"), lax.axis_index("tp")
    x, z = ctx // nz, ctx % nz
    y, core = tp // 2, tp % 2
    following, preceding = ((ctx + 1) % n_ctx, tp), ((ctx + n_ctx - 1) % n_ctx, tp)
    x_next = {1: ((x + 1) % nx * nz + z, tp), -1: ((x + nx - 1) % nx * nz + z, tp)}
    y_next = {1: (ctx, (y + 1) % ny * 2 + core), -1: (ctx, (y + ny - 1) % ny * 2 + core)}
    partner = (ctx, y * 2 + 1 - core)
    z_peer = {o: (x * nz + (z + o) % nz, tp) for o in range(1, nz)}
    chunk_x, chunk_y = gt_s.shape[0] // nx, wt_s.shape[1]
    piece = chunk_x // nz

    loads = [pltpu.make_async_copy(src, dst, load_sem.at[i]) for i, (src, dst) in enumerate(
        [(k_in, k_s.at[0]), (q_in, q_s), (doc_in, doc), (v_in, v_s.at[0]), (g_in, g_s), (w_in, w_s)])]
    for load in loads:
        load.start()
    barrier = pltpu.get_barrier_semaphore()
    beside = [*x_next.values(), *y_next.values(), partner]
    for device in [preceding, *beside]:
        pl.semaphore_signal(barrier, inc=1, device_id=device, device_id_type=MESH)
    pl.semaphore_wait(barrier, 1 + len(beside))

    def send(src, dst, snd, rcv, device):
        copy = pltpu.make_async_remote_copy(src_ref=src, dst_ref=dst, send_sem=snd, recv_sem=rcv, device_id=device,
                                            device_id_type=MESH)
        copy.start()
        return copy

    k_copy, v_copy = {}, {}

    def pass_k(d):
        k_copy[d] = send(k_in if d == 0 else k_s.at[d], k_s.at[d + 1], k_snd.at[d], k_rcv.at[d], following)

    def pass_v(d):
        v_copy[d] = send(v_in if d == 0 else v_s.at[d], v_s.at[d + 1], v_snd.at[d], v_rcv.at[d], following)

    pass_k(0)
    pass_v(0)
    for load in loads[:3]:
        load.wait()

    own_doc = doc[ctx]
    bias = [None] + [
        jnp.where((ctx >= d) & (doc[(ctx + n_ctx - d) % n_ctx] == own_doc), 0.0, HIDDEN).astype(F32)
        for d in range(1, REACH + 1)
    ]
    size = q_s.shape[0]
    key_at = lax.broadcasted_iota(jnp.int32, (size, size), 0)
    query_at = lax.broadcasted_iota(jnp.int32, (size, size), 1)

    def head(ref, h):
        return ref[:, h * HEAD:(h + 1) * HEAD]

    top, top_at, total, acc = {}, {}, {}, {}

    def attend(d):
        for h in range(HEADS):
            s = dot(k_s[d], head(q_s, h), 1, 1)
            if d == 0:
                s = jnp.where(key_at <= query_at, s, HIDDEN)
            if d == REACH:
                s = jnp.where(key_at > query_at, s, HIDDEN)
            most = jnp.max(s, axis=0, keepdims=True) * EXPONENT
            if d > 0:
                most = jnp.maximum(top[h], most + bias[d])
            p = jnp.exp2(s * EXPONENT - (most if d == 0 else most - bias[d]))
            p_s[d, h] = p
            rows = jnp.sum(p, axis=0, keepdims=True)
            if d == 0:
                total[h] = rows
            else:
                fade = jnp.exp2(top[h] - most)
                total[h] = total[h] * fade + rows
                acc[h] = acc[h] * fade
            top[h] = top_at[d, h] = most

    def weigh(d, heads=range(HEADS)):
        for h in heads:
            part = dot(v_s[d], p_s[d, h].astype(BF16), 0, 0)
            acc[h] = part if d == 0 else acc[h] + part

    def value_side(d):
        for h in range(HEADS):
            dp_s[d, h] = dot(v_s[d], head(do_s, h), 1, 1)

    def turn(src, dst):
        for j in range(src.shape[1] // 128):
            dst[j * 128:(j + 1) * 128, :] = src[:, j * 128:(j + 1) * 128].T.astype(dst.dtype)

    attend(0)
    for load in loads[3:]:
        load.wait()
    weigh(0)
    for d in range(1, REACH + 1):
        k_copy[d - 1].wait_recv()
        if d < REACH:
            pass_k(d)
        attend(d)
        v_copy[d - 1].wait_recv()
        if d < REACH:
            pass_v(d)
            weigh(d)
        if d == 1:
            do_s[...] = dot(g_s[...], w_s[...], 1, 1).astype(BF16)
            dot_s[...] = dot(w_s[...], g_s[...], 1, 1).astype(BF16)
        if d == 2:
            turn(g_s, gt_s)
        if d == 3:
            turn(w_s, wf_s)
            for i in range(wt_s.shape[0]):
                wt_s[i] = wf_s[i * chunk_y:(i + 1) * chunk_y, :].astype(BF16)
            for block in range(REACH):
                value_side(block)

    for d in range(1, REACH + 1):
        pl.semaphore_signal(z_ready, inc=1, device_id=((ctx + n_ctx - d) % n_ctx, tp), device_id_type=MESH)

    share, delta = {}, {}

    def conclude(h):
        weigh(REACH, [h])
        share[h] = 1.0 / total[h]
        attn = (acc[h] * share[h]).astype(BF16)
        at_s[h * HEAD:(h + 1) * HEAD, :] = attn
        delta[h] = jnp.sum(attn.astype(F32) * dot_s[h * HEAD:(h + 1) * HEAD, :].astype(F32), axis=0, keepdims=True)

    def weight_term(at, half):
        rows = gt_s[pl.ds(pl.multiple_of(at * chunk_x, 16), chunk_x), :]
        return dot(rows, at_s[half * 128:(half + 1) * 128, :], 1, 1)

    def output_term(at, half):
        return dot(wt_s[at * 2 + core], at_s[:, half * 128:(half + 1) * 128], 1, 0)

    x_slot, x_len = ring_slots(nx)
    y_slot, y_len = ring_slots(ny)
    chains = {"x": (weight_term, x, nx, x_next, xs, xr, x_snd, x_rcv, x_slot, x_len, {}),
              "y": (output_term, y, ny, y_next, ys, yr, y_snd, y_rcv, y_slot, y_len, {})}

    core_copies = {}

    def share_terms():
        for o in sorted(range(ny), key=lambda o: -min(o, ny - o)):
            cs[o] = dot(wt_s[(y + o) % ny * 2 + 1 - core], at_s[...], 1, 0).astype(BF16)
            core_copies[o] = send(cs.at[o], cr.at[o], c_snd.at[o], c_rcv.at[o], partner)

    arrived_terms = set()

    def chip_term(o, half):
        part = output_term((y + o) % ny, half)
        if o not in arrived_terms:
            core_copies[o].wait_recv()
            arrived_terms.add(o)
        return part + cr[o, :, half * 128:(half + 1) * 128].astype(F32)

    def chain_step(name, half, step):
        term, me, n, neighbour, out, arrived, snd, rcv, slot, length, copies = chains[name]
        for way in (1, -1):
            if step > length[half, way]:
                continue
            off = way * (length[half, way] - step + 1) % n
            part = chip_term(off, half) if name == "y" else term((me + off) % n, half)
            if step > 1:
                before = half, way, step - 1
                copies[before].wait_recv()
                part = part + arrived[slot[before]].astype(F32)
            now = slot[half, way, step]
            out[now] = part.astype(BF16)
            copies[half, way, step] = send(out.at[now], arrived.at[now], snd.at[now], rcv.at[now], neighbour[way])

    def chain_end(name, half):
        term, me, n, neighbour, out, arrived, snd, rcv, slot, length, copies = chains[name]
        part = chip_term(0, half) if name == "y" else term(me, half)
        for way in (1, -1):
            steps = length[half, way]
            if steps:
                copies[half, way, steps].wait_recv()
                part = part + arrived[slot[half, way, steps]].astype(F32)
        return part

    query_part, grad_copies = {}, {}

    def backward(d):
        key_part = value_part = None
        for h in range(HEADS):
            probs = p_s[d, h] * (jnp.exp2(top_at[d, h] - top[h]) * share[h])
            d_scores = (probs * (dp_s[d, h] - delta[h])).astype(BF16)
            to_value = dot(probs.astype(BF16), head(do_s, h), 1, 0)
            to_key = dot(d_scores, head(q_s, h), 1, 0)
            to_query = dot(k_s[d], d_scores, 0, 0)
            query_part[h] = query_part[h] + to_query if h in query_part else to_query
            key_part = to_key if key_part is None else key_part + to_key
            value_part = to_value if value_part is None else value_part + to_value
        return key_part, value_part

    def grad_step(step, kind, part):
        if step > 1:
            grad_copies[step - 1, kind].wait_recv()
            part = part + gr[step - 2, kind].astype(F32)
        gs[step - 1, kind] = part.astype(BF16)
        grad_copies[step, kind] = send(gs.at[step - 1, kind], gr.at[step - 1, kind], g_snd.at[step - 1, kind],
                                       g_rcv.at[step - 1, kind], preceding)

    steps_x, steps_y = max(x_len.values()), max(y_len.values())
    for step in range(1, max(steps_x, REACH) + 1):
        for half in (0, 1):
            if step == 1:
                conclude(half)
            if step <= steps_x:
                chain_step("x", half, step)
        if step == 2:
            for o in range(nz // 2 + 1, nz):
                pl.semaphore_signal(z_ready, inc=1, device_id=z_peer[o], device_id_type=MESH)
        if step == 1:
            share_terms()
            value_side(REACH)
        elif step - 1 <= steps_y:
            for half in (0, 1):
                chain_step("y", half, step - 1)
        if step <= REACH:
            key_part, value_part = backward(REACH + 1 - step)
            grad_step(step, 0, key_part)
            grad_step(step, 1, value_part)

    key_part, value_part = backward(0)
    for h in range(HEADS):
        dq_o[:, h * HEAD:(h + 1) * HEAD] = (query_part[h] * query_scale).T.astype(BF16)
    z_copies = {}
    za[chunk_x:, :] = jnp.zeros((za.shape[0] - chunk_x, 128), F32)
    for half in (0, 1):
        za[0:chunk_x, :] = chain_end("x", half)
        for i in range(nz):
            rows = za[i * piece:i * piece + zf.shape[2], :]
            zf[half, i] = rows
            zs[half, i] = rows.astype(BF16)
        if half == 0:
            pl.semaphore_wait(z_ready, REACH + nz - 1 - nz // 2)
        for o in sorted(range(1, nz), key=lambda o: -min(o, nz - o)):
            z_copies[half, o] = send(zs.at[half, (z + o) % nz], zr.at[half, o - 1], z_snd.at[half, o - 1],
                                     z_rcv.at[half, o - 1], z_peer[o])
    for step in range(max(steps_x, REACH), steps_y + 1):
        for half in (0, 1):
            chain_step("y", half, step)
    for half in (0, 1):
        out_o[:, half * 128:(half + 1) * 128] = chain_end("y", half).astype(BF16)
    grad_copies[REACH, 0].wait_recv()
    dk_o[...] = ((key_part + gr[REACH - 1, 0].astype(F32)) * query_scale).astype(BF16)
    grad_copies[REACH, 1].wait_recv()
    dv_o[...] = (value_part + gr[REACH - 1, 1].astype(F32)).astype(BF16)
    for half in (0, 1):
        part = zf[half, z]
        for o in range(1, nz):
            z_copies[half, o].wait_recv()
            part = part + zr[half, o - 1].astype(F32)
        dw_o[:, half * 128:(half + 1) * 128] = part[:piece]
    for copies in (k_copy, v_copy, chains["x"][-1], chains["y"][-1], grad_copies, z_copies, core_copies):
        for copy in copies.values():
            copy.wait_send()


def hand_over(*refs):
    for src, dst in zip(refs[:5], refs[5:]):
        dst[...] = src[...]


def local(nx, ny, nz, queries, keys, values, out_weight, out_grad, block_doc):
    size, width = queries.shape
    features = out_weight.shape[1]
    chunk_x, chunk_y = features // nx, features // (2 * ny)
    piece = chunk_x // nz
    piece_rows = -(-piece // 16) * 16
    x_slots, y_slots = len(ring_slots(nx)[0]), len(ring_slots(ny)[0])
    DMA = pltpu.SemaphoreType.DMA
    V = pltpu.VMEM
    scratch = [
        pltpu.SMEM(block_doc.shape, jnp.int32),
        V((size, width), BF16), V((REACH + 1, size, HEAD), BF16), V((REACH + 1, size, HEAD), BF16),
        V((width, features), BF16), V((size, features), BF16), V((features, width), F32), V((2 * ny, chunk_y, width), BF16),
        V((features, size), BF16),
        V((REACH + 1, HEADS, size, size), F32), V((REACH + 1, HEADS, size, size), F32),
        V((width, size), BF16), V((size, width), BF16), V((width, size), BF16),
        V((x_slots, chunk_x, 128), BF16), V((x_slots, chunk_x, 128), BF16),
        V((y_slots, chunk_y, 128), BF16), V((y_slots, chunk_y, 128), BF16),
        V((REACH, 2, size, HEAD), BF16), V((REACH, 2, size, HEAD), BF16),
        V((chunk_x + piece_rows, 128), F32), V((2, nz, piece_rows, 128), F32), V((2, nz, piece_rows, 128), BF16),
        V((2, max(nz - 1, 1), piece_rows, 128), BF16),
        V((ny, chunk_y, size), BF16), V((ny, chunk_y, size), BF16),
        DMA((6,)), DMA((REACH,)), DMA((REACH,)), DMA((REACH,)), DMA((REACH,)),
        DMA((x_slots,)), DMA((x_slots,)), DMA((y_slots,)), DMA((y_slots,)),
        DMA((REACH, 2)), DMA((REACH, 2)), DMA((2, nz - 1)), DMA((2, nz - 1)), DMA((ny,)), DMA((ny,)),
        pltpu.SemaphoreType.REGULAR,
    ]
    in_hbm, vmem = pl.BlockSpec(memory_space=pltpu.HBM), pl.BlockSpec(memory_space=pltpu.VMEM)
    results = pl.pallas_call(
        functools.partial(kernel, nx, ny, nz),
        out_shape=[
            jax.ShapeDtypeStruct((chunk_y, size), BF16),
            jax.ShapeDtypeStruct((size, width), BF16),
            jax.ShapeDtypeStruct((size, HEAD), BF16),
            jax.ShapeDtypeStruct((size, HEAD), BF16),
            jax.ShapeDtypeStruct((piece, width), F32),
        ],
        in_specs=[in_hbm] * 6,
        out_specs=[vmem] * 5,
        scratch_shapes=scratch,
        compiler_params=pltpu.CompilerParams(collective_id=0, has_side_effects=True, vmem_limit_bytes=40 << 20),
        name="layer",
    )(*[pltpu.with_memory_space_constraint(a, pltpu.HBM) for a in (block_doc, queries, keys, values, out_weight, out_grad)])
    out, dq, dk, dv, dw = pl.pallas_call(
        hand_over,
        out_shape=[jax.ShapeDtypeStruct(r.shape, r.dtype) for r in results],
        in_specs=[vmem] * 5,
        out_specs=[vmem] * 5,
        compiler_params=pltpu.CompilerParams(vmem_limit_bytes=8 << 20),
        name="hand_over",
    )(*results)
    return out.T, dq, dk, dv, dw.T


def solution(mesh, nx=8, ny=8, nz=8):
    placed = (P("ctx", "tp"), P("ctx", "tp"), P("ctx", "tp"), P("tp", None), P("ctx", None), P())
    return jax.shard_map(
        functools.partial(local, nx, ny, nz),
        mesh=mesh,
        in_specs=placed,
        out_specs=(P("ctx", "tp"), P("ctx", "tp"), P("ctx", "tp"), P("ctx", "tp"), P("tp", "ctx")),
        check_vma=False,
    )
```
